256 devices in a mesh: grid: 32 (over y_lo, z, core), orb: 8 (over y_hi, x).
Axes of the slice: x: 4, y: 4 (y_hi: 2, y_lo: 2; y = y_hi * 2 + y_lo), z: 8, core: 2. Of those that a mesh axis runs over, the one named last changes fastest.
Arguments:
- orbitals: bfloat16 [64, 1769472], P('orb', 'grid'), may hold values from -6 to 6
- potential: float32 [1769472], P('grid'), may hold values from -2 to 0
- projector_atom: int32 [49152], P('grid'), may hold values from 0 to 127, as said below
- projector_cell: int32 [49152], P('grid'), may hold values from 0 to 55295
- projector_value: float32 [49152], P('grid'), may hold values from -1.5 to 1.5
- atom_strength: float32 [128], replicated, may hold values from 0.25 to 2
- ritz_rotation: bfloat16 [4, 8, 128], P(None, None, 'orb'), may hold values from -1 to 1
- panel_owner: int32 [4], replicated, may hold values from 0 to 7
Outputs:
- filtered: bfloat16 [64, 1769472], P('orb', 'grid')
- rotated: bfloat16 [128, 1769472], P('orb', 'grid')
The draws below stay inside these ranges and needn't reach their ends.
Inputs may be any that keep to these rules, and one draw needn't show every extreme that they name: `projector_atom`: the entries e of slab s (e // 1536 = s) name atoms of slabs s - 1, s and s + 1 only, slab t holding atoms t * 4 to (t + 1) * 4 - 1.
All inputs are finite; a program needn't handle non-finite values.
Results may differ from the reference program's by a relative error of at most 0.0049.
Values may be sent and summed in bfloat16 or wider, within the bound.
A program may use at most 128 MiB of HBM per device.

```python
import math
import jax
import jax.numpy as jnp
from jax import lax

NX = 96
NY = 96
REACH = 6
PANEL = 8
STEPS = 4
ATOM_DEV = 4
ENTRY_DEV = 1536
CELL_DEV = 55296
CELLS = 1769472
NORB = 64
RITZ = 128
NATOM = 128
ENTRIES = 49152
N_ORB = 8


def draw_projector_atom(key, part):
    slab_count = NATOM // ATOM_DEV
    owner_slab = jnp.arange(ENTRIES, dtype=jnp.int32) // ENTRY_DEV
    offset_key, member_key = jax.random.split(key)
    offsets = jax.random.randint(offset_key, (ENTRIES,), -1, 2, dtype=jnp.int32)
    target = jnp.clip(owner_slab + offsets, 0, slab_count - 1)
    member = jax.random.randint(member_key, (ENTRIES,), 0, ATOM_DEV, dtype=jnp.int32)
    return (target * ATOM_DEV + member).astype(jnp.int32)


def with_ends(drawn, rng, smallest, largest):
    extent = drawn.shape
    place = [jax.random.randint(jax.random.fold_in(rng, axis), (), 0, extent[axis]) for axis in range(len(extent))]
    drawn = drawn.at[tuple(place)].set(smallest)
    longest = extent.index(max(extent))
    place[longest] = (place[longest] + 1) % extent[longest]
    return drawn.at[tuple(place)].set(largest)


def steps_of(key, extent, cuts, smallest, largest):
    def one(axis_at, parts):
        heights = jax.random.uniform(jax.random.fold_in(jax.random.fold_in(key, 6), axis_at), (parts,), jnp.float32, smallest / len(cuts), largest / len(cuts))
        return jnp.repeat(jnp.exp(heights), extent[axis_at] // parts).reshape((-1,) + (1,) * (len(extent) - axis_at - 1))

    factor_of = one(*cuts[0])
    for cut in cuts[1:]:
        factor_of = factor_of * one(*cut)
    return factor_of


def normal_values(own_key, shape, width, most, shards=(), kind=jnp.bfloat16):
    factor_of = steps_of(own_key, shape, shards, -0.22, 0.18) if shards else 1.0
    values = jax.random.normal(own_key, shape, jnp.float32) * width * factor_of
    return jnp.minimum(jnp.maximum(values, -most), most).astype(kind)


def setup_inputs(seed: int = 0) -> dict:
    streams_of = jax.random.split(jax.random.key(seed), 9)
    orbitals = normal_values(streams_of[0], (NORB, CELLS), 1.0, 6.0, ((0, 8), (1, 32)))
    potential = jnp.clip(-2.0 + 2.0 * jax.random.uniform(streams_of[1], (CELLS,), jnp.float32) ** steps_of(streams_of[1], (CELLS,), ((0, 32),), -0.2, 0.2), -2.0, 0.0)
    projector_atom = draw_projector_atom(jax.random.fold_in(streams_of[8], 71), 0)
    projector_cell = with_ends(jax.random.randint(streams_of[3], (ENTRIES,), 0, CELL_DEV), jax.random.fold_in(streams_of[3], 1), 0, CELL_DEV - 1).astype(jnp.int32)
    projector_value = normal_values(streams_of[4], (ENTRIES,), 0.25, 1.5, ((0, 32),), jnp.float32)
    atom_strength = jnp.clip(jnp.exp(jax.random.uniform(streams_of[5], (NATOM,), jnp.float32, math.log(0.25), math.log(2.0))), 0.25, 2.0)
    ritz_rotation = normal_values(streams_of[6], (STEPS, PANEL, RITZ), (STEPS * PANEL) ** -0.5, 1.0, ((2, 8),))
    panel_owner = with_ends(jax.random.randint(streams_of[7], (STEPS,), 0, N_ORB), jax.random.fold_in(streams_of[7], 1), 0, N_ORB - 1).astype(jnp.int32)
    return {"orbitals": orbitals, "potential": potential, "projector_atom": projector_atom, "projector_cell": projector_cell, "projector_value": projector_value, "atom_strength": atom_strength, "ritz_rotation": ritz_rotation, "panel_owner": panel_owner}


stencil_weights = (-5369.0 / 1800.0, 12.0 / 7.0, -15.0 / 56.0, 10.0 / 189.0, -1.0 / 112.0, 2.0 / 1925.0, -1.0 / 16632.0)
cheb_center = 6.0
cheb_half = 6.0


def laplace(extended, cell_count, column_pos, row_pos):
    plane_cells = NX * NY
    margin = REACH * plane_cells
    middle = extended[:, margin:margin + cell_count].astype(jnp.float32)
    summed = 3.0 * stencil_weights[0] * middle
    for distance in range(1, REACH + 1):
        plane_jump = distance * plane_cells
        row_jump = distance * NX
        upper_plane = extended[:, margin + plane_jump:margin + plane_jump + cell_count].astype(jnp.float32)
        lower_plane = extended[:, margin - plane_jump:margin - plane_jump + cell_count].astype(jnp.float32)
        row_after = extended[:, margin + row_jump:margin + row_jump + cell_count].astype(jnp.float32)
        row_before = extended[:, margin - row_jump:margin - row_jump + cell_count].astype(jnp.float32)
        cell_after = extended[:, margin + distance:margin + distance + cell_count].astype(jnp.float32)
        cell_before = extended[:, margin - distance:margin - distance + cell_count].astype(jnp.float32)
        neighbours = upper_plane + lower_plane
        neighbours = neighbours + jnp.where(row_pos + distance < NY, row_after, 0.0) + jnp.where(row_pos >= distance, row_before, 0.0)
        neighbours = neighbours + jnp.where(column_pos + distance < NX, cell_after, 0.0) + jnp.where(column_pos >= distance, cell_before, 0.0)
        summed = summed + stencil_weights[distance] * neighbours
    return middle, summed


def nonlocal_part(middle, cell_index, projector_atom, projector_value, atom_strength):
    gathered = jnp.take(middle, cell_index, axis=1)
    weighted = gathered * projector_value
    atom_sums = jax.ops.segment_sum(weighted.T, projector_atom, num_segments=NATOM)
    scaled = atom_sums * atom_strength[:, None]
    spread = jnp.take(scaled, projector_atom, axis=0).T * projector_value
    return jnp.zeros_like(middle).at[:, cell_index].add(spread)


def hamiltonian(field, potential, cell_index, projector_atom, projector_value, atom_strength, column_pos, row_pos):
    margin = REACH * NX * NY
    extended = jnp.pad(field, ((0, 0), (margin, margin)))
    middle, summed = laplace(extended, field.shape[1], column_pos, row_pos)
    nonlocal_term = nonlocal_part(middle, cell_index, projector_atom, projector_value, atom_strength)
    return -0.5 * summed + potential * middle + nonlocal_term


def reference(orbitals, potential, projector_atom, projector_cell, projector_value, atom_strength, ritz_rotation, panel_owner):
    cell_ids = jnp.arange(CELLS, dtype=jnp.int32)
    column_pos = cell_ids % NX
    row_pos = (cell_ids // NX) % NY
    cell_index = (jnp.arange(ENTRIES, dtype=jnp.int32) // ENTRY_DEV) * CELL_DEV + projector_cell

    def apply_field(field):
        return hamiltonian(field, potential, cell_index, projector_atom, projector_value, atom_strength, column_pos, row_pos)

    def filter_panel(panel):
        initial = panel.astype(jnp.float32)
        first_image = apply_field(panel)
        step_field = (first_image - cheb_center * initial) / cheb_half
        second = apply_field(step_field)
        return (2.0 * (second - cheb_center * step_field) / cheb_half - initial).astype(jnp.bfloat16)

    filtered = lax.map(filter_panel, orbitals.reshape(N_ORB, PANEL, CELLS)).reshape(NORB, CELLS)
    stacked = jnp.take(filtered.reshape(N_ORB, PANEL, CELLS), panel_owner, axis=0).reshape(STEPS * PANEL, CELLS)
    rotation_rows = ritz_rotation.reshape(STEPS * PANEL, RITZ)
    row_blocks = rotation_rows.T.reshape(8, RITZ // 8, STEPS * PANEL)
    rotated = lax.map(lambda block_rows: jnp.dot(block_rows, stacked, preferred_element_type=jnp.float32).astype(jnp.bfloat16), row_blocks)
    return filtered, rotated.reshape(RITZ, CELLS)
```

```python
import functools

import jax
import jax.numpy as jnp
import ml_dtypes
import numpy as np
from jax import lax
from jax.experimental import pallas as pl
from jax.experimental.pallas import tpu as pltpu
from jax.sharding import PartitionSpec as P

NX = 96
NY = 96
REACH = 6
ATOM_DEV = 4
PLANE = NX * NY
DEPTH = 6
PANEL = 8
ROWS = DEPTH * PANEL
BLOCK = 256
BLOCKS = PLANE // BLOCK
PAD = 640
WINDOW = BLOCK + 2 * PAD
PHASES = 3
CHUNKS = 3
CHUNK = PLANE // CHUNKS
CHUNK_BLOCKS = CHUNK // BLOCK
ATOM_SLOTS = 16
COARSE = 512
FLOAT = jnp.float32
HALF = jnp.bfloat16
MESH = pl.DeviceIdType.MESH

stencil_weights = (
    -5369.0 / 1800.0,
    12.0 / 7.0,
    -15.0 / 56.0,
    10.0 / 189.0,
    -1.0 / 112.0,
    2.0 / 1925.0,
    -1.0 / 16632.0,
)
cheb_center = 6.0
cheb_half = 6.0
unit = stencil_weights[1]


def plane_bands():
    bands = np.zeros((PHASES, WINDOW, BLOCK), np.float32)
    for phase in range(PHASES):
        target = phase * BLOCK + np.arange(BLOCK)
        source = phase * BLOCK - PAD + np.arange(WINDOW)
        jump = source[:, None] - target[None, :]
        same_row = (source[:, None] // NX) == (target[None, :] // NX)
        for k in range(1, REACH + 1):
            weight = stencil_weights[k] / unit
            bands[phase] += weight * ((np.abs(jump) == k) & same_row)
            bands[phase] += weight * (np.abs(jump) == k * NX)
    return bands.astype(ml_dtypes.bfloat16)


def depth_band():
    band = np.zeros((DEPTH, 3 * DEPTH), np.float32)
    for z in range(DEPTH):
        for k in range(1, REACH + 1):
            band[z, DEPTH + z - k] += stencil_weights[k] / unit
            band[z, DEPTH + z + k] += stencil_weights[k] / unit
    return np.kron(band, np.eye(PANEL, dtype=np.float32))


def contract_last(left, right):
    return lax.dot_general(left, right, (((1,), (1,)), ((), ())), preferred_element_type=FLOAT)


def dot(left, right):
    return jnp.dot(left, right, preferred_element_type=FLOAT)


def filter_kernel(
    slabs,
    orbitals,
    potential,
    atom,
    cell,
    value,
    strength,
    depth_weights,
    bands_hbm,
    filtered,
    filtered_rows,
    bands,
    stack,
    padded,
    planar,
    step,
    picks,
    spots,
    table,
    sums_out,
    sums_in,
    band_sem,
    halo_send,
    halo_recv,
    sums_send,
    sums_recv,
):
    me = lax.axis_index("grid")
    after, before = lax.rem(me + 1, slabs), lax.rem(me + slabs - 1, slabs)
    after2, before2 = lax.rem(me + 2, slabs), lax.rem(me + slabs - 2, slabs)
    barrier = pltpu.get_barrier_semaphore()
    for other in (after, before, after2, before2):
        pl.semaphore_signal(barrier, inc=1, device_id={"grid": other}, device_id_type=MESH)
    band_copy = pltpu.make_async_copy(bands_hbm, bands, band_sem)
    band_copy.start()

    def halo_copies(stage, chunk):
        columns = pl.ds(chunk * CHUNK, CHUNK)
        own = stack.at[stage, pl.ds(ROWS, ROWS), columns]
        return [
            pltpu.make_async_remote_copy(
                src_ref=own,
                dst_ref=stack.at[stage, pl.ds(place, ROWS), columns],
                send_sem=halo_send.at[stage, side, chunk],
                recv_sem=halo_recv.at[stage, side, chunk],
                device_id={"grid": other},
                device_id_type=MESH,
            )
            for side, (other, place) in enumerate(((after, 0), (before, 2 * ROWS)))
        ]

    def store_own(stage, j, rows):
        stack[stage, pl.ds(ROWS, ROWS), pl.ds(pl.multiple_of(j * BLOCK, BLOCK), BLOCK)] = rows
        padded[stage, :, pl.ds(pl.multiple_of(PAD + j * BLOCK, 128), BLOCK)] = rows

    for stage in range(2):
        padded[stage, :, pl.ds(0, PAD)] = jnp.zeros((ROWS, PAD), HALF)
        padded[stage, :, pl.ds(PAD + PLANE, PAD)] = jnp.zeros((ROWS, PAD), HALF)

    for chunk in range(CHUNKS):

        def take_block(i, carry, chunk=chunk):
            j = chunk * CHUNK_BLOCKS + i
            planes = [
                orbitals[:, pl.ds(pl.multiple_of(z * PLANE + j * BLOCK, BLOCK), BLOCK)].astype(FLOAT)
                for z in range(DEPTH)
            ]
            store_own(0, j, jnp.concatenate(planes, 0).astype(HALF))
            return carry

        lax.fori_loop(0, CHUNK_BLOCKS, take_block, 0)
        if chunk == 0:
            pl.semaphore_wait(barrier, 4)
        for copy in halo_copies(0, chunk):
            copy.start()

    cells = cell[...]
    plane_of = jnp.zeros_like(cells)
    for z in range(1, DEPTH):
        plane_of = plane_of + (cells >= z * PLANE).astype(jnp.int32)
    in_plane = cells - plane_of * PLANE
    slot = atom[...] - (me - 1) * ATOM_DEV
    coarse_key = (in_plane >> 9) * (DEPTH * ATOM_SLOTS) + plane_of * ATOM_SLOTS + slot
    fine_key = in_plane & (COARSE - 1)
    entries = cells.shape[1]
    values = value[...]
    high = values.astype(HALF).astype(FLOAT)
    low = values - high

    def fill_spots(i, carry):
        row = pl.multiple_of(i * 32, 32)
        here = (lax.broadcasted_iota(jnp.int32, (32, entries), 0) + row) == fine_key
        spots[pl.ds(row, 32), :] = jnp.where(here, high, 0.0).astype(HALF)
        spots[pl.ds(row + COARSE, 32), :] = jnp.where(here, low, 0.0).astype(HALF)
        return carry

    lax.fori_loop(0, COARSE // 32, fill_spots, 0)
    table_rows = DEPTH * ATOM_SLOTS
    for start in (table_rows, 128 + table_rows):
        table[pl.ds(start, 128 - table_rows), :] = jnp.zeros((128 - table_rows, PLANE), HALF)
    groups = PLANE // COARSE
    per_round = 6
    picked = per_round * table_rows

    def fill_table(turn, carry):
        def fill_picks(i, inner):
            row = pl.multiple_of(i * 32, 32)
            here = (
                lax.broadcasted_iota(jnp.int32, (32, entries), 0) + (row + turn * picked)
            ) == coarse_key
            picks[pl.ds(row, 32), :] = jnp.where(here, 1.0, 0.0).astype(HALF)
            return inner

        lax.fori_loop(0, picked // 32, fill_picks, 0)
        full = contract_last(picks[...], spots[pl.ds(0, COARSE), :]) + contract_last(
            picks[...], spots[pl.ds(COARSE, COARSE), :]
        )
        for i in range(per_round):
            part = full[i * table_rows : (i + 1) * table_rows]
            rounded = part.astype(HALF)
            columns = pl.ds(pl.multiple_of((turn * per_round + i) * COARSE, COARSE), COARSE)
            table[pl.ds(0, table_rows), columns] = rounded
            table[pl.ds(128, table_rows), columns] = (part - rounded.astype(FLOAT)).astype(HALF)
        return carry

    lax.fori_loop(0, groups // per_round, fill_table, 0)
    band_copy.wait()

    lanes = lax.broadcasted_iota(jnp.int32, (PANEL, 128), 1)
    near_strength = pltpu.roll(
        jnp.broadcast_to(strength[...], (PANEL, 128)),
        lax.rem(128 + ATOM_DEV - me * ATOM_DEV, 128),
        1,
    )
    column_of = lax.broadcasted_iota(jnp.int32, (ROWS, 3 * ROWS), 1)
    has_before = (me > 0).astype(FLOAT)
    has_after = (me < slabs - 1).astype(FLOAT)
    keep = jnp.where(
        column_of < ROWS, has_before, jnp.where(column_of >= 2 * ROWS, has_after, 1.0)
    )
    across = (depth_weights[...] * keep).astype(HALF)
    plane_lanes = [(lanes >= z * ATOM_SLOTS) & (lanes < (z + 1) * ATOM_SLOTS) for z in range(DEPTH)]
    partners = ((after, 124), (before, 4), (after2, 120), (before2, 8))

    def send_sums(stage):
        def add_part(i, total):
            columns = pl.ds(pl.multiple_of(i * 1024, 1024), 1024)
            return total + contract_last(
                stack[stage, pl.ds(ROWS, ROWS), columns], table[:, columns]
            )

        found = lax.fori_loop(0, PLANE // 1024, add_part, jnp.zeros((ROWS, 256), FLOAT))
        both = found[:, :128] + found[:, 128:]
        own = jnp.zeros((PANEL, 128), FLOAT)
        for z in range(DEPTH):
            part = jnp.where(plane_lanes[z], both[z * PANEL : (z + 1) * PANEL], 0.0)
            own = own + (part if z == 0 else pltpu.roll(part, 128 - z * ATOM_SLOTS, 1))
        sums_out[stage] = own
        copies = [
            pltpu.make_async_remote_copy(
                src_ref=sums_out.at[stage],
                dst_ref=sums_in.at[stage, k],
                send_sem=sums_send.at[stage, k],
                recv_sem=sums_recv.at[stage, k],
                device_id={"grid": other},
                device_id_type=MESH,
            )
            for k, (other, _) in enumerate(partners)
        ]
        for copy in copies:
            copy.start()
        return copies

    def planar_part(stage):
        for phase in range(PHASES):
            windows = [
                padded[stage, :, pl.ds((i * PHASES + phase) * BLOCK, WINDOW)]
                for i in range(BLOCKS // PHASES)
            ]
            product = dot(jnp.concatenate(windows, 0), bands[phase])
            for i in range(BLOCKS // PHASES):
                planar[:, pl.ds((i * PHASES + phase) * BLOCK, BLOCK)] = product[
                    i * ROWS : (i + 1) * ROWS
                ]

    def coupling(stage, copies):
        for copy in copies:
            copy.wait()
        total = sums_out[stage]
        for k, (_, turn) in enumerate(partners):
            total = total + pltpu.roll(sums_in[stage, k], turn, 1)
        scaled = jnp.where(plane_lanes[0], total * near_strength, 0.0)
        blocks = [
            scaled if z == 0 else pltpu.roll(scaled, z * ATOM_SLOTS, 1) for z in range(DEPTH)
        ]
        spread = jnp.concatenate(blocks, 0)
        rounded = spread.astype(HALF)
        rest = (spread - rounded.astype(FLOAT)).astype(HALF)
        return jnp.concatenate([rounded, rounded], 1), rest

    def image(stage, j, main, rest, middle):
        columns = pl.ds(pl.multiple_of(j * BLOCK, BLOCK), BLOCK)
        neighbours = planar[:, columns] + dot(across, stack[stage, :, columns])
        nonlocal_part = dot(main, table[:, columns]) + dot(rest, table[pl.ds(0, 128), columns])
        rows = []
        for z in range(DEPTH):
            halves = [
                jnp.broadcast_to(
                    potential[pl.ds(z * (PLANE // 128) + j * (BLOCK // 128) + h, 1), :], (PANEL, 128)
                )
                for h in range(BLOCK // 128)
            ]
            rows.append(jnp.concatenate(halves, 1))
        local = (jnp.concatenate(rows, 0) - (1.5 * stencil_weights[0] + cheb_center)) * (
            1.0 / cheb_half
        )
        return (
            middle * local
            - (0.5 * unit / cheb_half) * neighbours
            + nonlocal_part * (1.0 / cheb_half)
        )

    sums = send_sums(0)
    planar_part(0)
    main, rest = coupling(0, sums)
    for chunk in range(CHUNKS):
        for copy in halo_copies(0, chunk):
            copy.wait()

        def first_block(i, carry, chunk=chunk):
            j = chunk * CHUNK_BLOCKS + i
            columns = pl.ds(pl.multiple_of(j * BLOCK, BLOCK), BLOCK)
            middle = stack[0, pl.ds(ROWS, ROWS), columns].astype(FLOAT)
            field = image(0, j, main, rest, middle)
            step[:, columns] = field
            store_own(1, j, field.astype(HALF))
            return carry

        lax.fori_loop(0, CHUNK_BLOCKS, first_block, 0)
        for copy in halo_copies(1, chunk):
            copy.start()

    sums = send_sums(1)
    planar_part(1)
    main, rest = coupling(1, sums)
    for chunk in range(CHUNKS):
        for copy in halo_copies(1, chunk):
            copy.wait()

        def second_block(i, carry, chunk=chunk):
            j = chunk * CHUNK_BLOCKS + i
            columns = pl.ds(pl.multiple_of(j * BLOCK, BLOCK), BLOCK)
            initial = stack[0, pl.ds(ROWS, ROWS), columns].astype(FLOAT)
            field = 2.0 * image(1, j, main, rest, step[:, columns]) - initial
            filtered_rows[:, columns] = field.astype(HALF)
            for z in range(DEPTH):
                filtered[:, pl.ds(pl.multiple_of(z * PLANE + j * BLOCK, BLOCK), BLOCK)] = field[
                    z * PANEL : (z + 1) * PANEL
                ].astype(HALF)
            return carry

        lax.fori_loop(0, CHUNK_BLOCKS, second_block, 0)


PIECES = 3


def rotate_kernel(
    panels,
    source_rows,
    own_rotation,
    spread_index,
    spread_plane,
    rotated,
    rotations,
    wide,
    gathered,
    products,
    landed,
    local_sem,
    rot_send,
    rot_recv,
    in_send,
    in_recv,
    out_send,
    out_recv,
):
    me = lax.axis_index("orb")
    width = PLANE // panels
    piece = width // PIECES
    columns_out = own_rotation.shape[0]
    barrier = pltpu.get_barrier_semaphore()
    others = [lax.rem(me + k, panels) for k in range(1, panels)]
    for other in others:
        pl.semaphore_signal(barrier, inc=1, device_id={"orb": other}, device_id_type=MESH)

    def at(index, size):
        return pl.ds(pl.multiple_of(index * size, size), size)

    def columns(owner, part):
        return pl.ds(pl.multiple_of(owner * width + part * piece, 128), piece)

    own_copies = [
        pltpu.make_async_copy(
            source_rows.at[:, columns(me, part)],
            gathered.at[part, at(me, ROWS), :],
            local_sem.at[part],
        )
        for part in range(PIECES)
    ]
    own_copies.append(
        pltpu.make_async_copy(own_rotation, rotations.at[at(me, columns_out), :], local_sem.at[PIECES])
    )
    for copy in own_copies:
        copy.start()
    pl.semaphore_wait(barrier, panels - 1)
    rotation_copies = [
        pltpu.make_async_remote_copy(
            src_ref=own_rotation,
            dst_ref=rotations.at[at(me, columns_out), :],
            send_sem=rot_send.at[k],
            recv_sem=rot_recv.at[k],
            device_id={"orb": other},
            device_id_type=MESH,
        )
        for k, other in enumerate(others)
    ]
    panel_copies = [
        [
            pltpu.make_async_remote_copy(
                src_ref=source_rows.at[:, columns(other, part)],
                dst_ref=gathered.at[part, at(me, ROWS), :],
                send_sem=in_send.at[part, k],
                recv_sem=in_recv.at[part, k],
                device_id={"orb": other},
                device_id_type=MESH,
            )
            for k, other in enumerate(others)
        ]
        for part in range(PIECES)
    ]
    for copy in rotation_copies:
        copy.start()
    for part in range(PIECES):
        for copy in panel_copies[part]:
            copy.start()

    own_copies[PIECES].wait()
    for copy in rotation_copies:
        copy.wait()
    span = wide.shape[1]
    every = rotations[...]
    row_of = lax.broadcasted_iota(jnp.int32, (every.shape[1], span), 0)
    for z in range(DEPTH):
        chosen = (row_of == spread_index[...]) & (spread_plane[...] == z)
        product = dot(every, jnp.where(chosen, 1.0, 0.0).astype(HALF)).astype(HALF)
        for d in range(panels):
            wide[pl.ds((d * DEPTH + z) * columns_out, columns_out), :] = product[
                d * columns_out : (d + 1) * columns_out
            ]

    deep = DEPTH * columns_out
    result_copies = []
    back_copies = []
    for part in range(PIECES):
        own_copies[part].wait()
        for copy in panel_copies[part]:
            copy.wait()
        operand = gathered[part]
        half = span // 2
        product = dot(wide[:, :half], operand) + dot(wide[:, half:], operand)
        products[part] = product.astype(HALF)
        copies = [
            pltpu.make_async_remote_copy(
                src_ref=products.at[part, at(other, deep), :],
                dst_ref=landed.at[:, columns(me, part)],
                send_sem=out_send.at[part, k],
                recv_sem=out_recv.at[part, k],
                device_id={"orb": other},
                device_id_type=MESH,
            )
            for k, other in enumerate(others)
        ]
        for copy in copies:
            copy.start()
        landed[:, columns(me, part)] = products[part, at(me, deep), :]
        result_copies.extend(copies)
    for copy in result_copies:
        copy.wait()
    for z in range(DEPTH):
        back = pltpu.make_async_copy(
            landed.at[pl.ds(z * columns_out, columns_out), :],
            rotated.at[:, pl.ds(z * PLANE, PLANE)],
            local_sem.at[z],
        )
        back.start()
        back_copies.append(back)
    for back in back_copies:
        back.wait()


def body(
    slabs,
    panels,
    orbitals,
    potential,
    projector_atom,
    projector_cell,
    projector_value,
    atom_strength,
    ritz_rotation,
    panel_owner,
):
    cell_count = orbitals.shape[1]
    entries = projector_atom.shape[0]
    in_vmem = pl.BlockSpec(memory_space=pltpu.VMEM)
    anywhere = pl.BlockSpec(memory_space=pl.ANY)
    dma = pltpu.SemaphoreType.DMA
    filtered, filtered_rows = pl.pallas_call(
        functools.partial(filter_kernel, slabs),
        out_shape=(
            jax.ShapeDtypeStruct(orbitals.shape, HALF),
            jax.ShapeDtypeStruct((ROWS, PLANE), HALF),
        ),
        in_specs=[in_vmem] * 7 + [anywhere],
        out_specs=(in_vmem, in_vmem),
        scratch_shapes=[
            pltpu.VMEM((PHASES, WINDOW, BLOCK), HALF),
            pltpu.VMEM((2, 3 * ROWS, PLANE), HALF),
            pltpu.VMEM((2, ROWS, PLANE + 2 * PAD), HALF),
            pltpu.VMEM((ROWS, PLANE), FLOAT),
            pltpu.VMEM((ROWS, PLANE), FLOAT),
            pltpu.VMEM((6 * DEPTH * ATOM_SLOTS, entries), HALF),
            pltpu.VMEM((2 * COARSE, entries), HALF),
            pltpu.VMEM((256, PLANE), HALF),
            pltpu.VMEM((2, PANEL, 128), FLOAT),
            pltpu.VMEM((2, 4, PANEL, 128), FLOAT),
            dma,
            dma((2, 2, CHUNKS)),
            dma((2, 2, CHUNKS)),
            dma((2, 4)),
            dma((2, 4)),
        ],
        compiler_params=pltpu.CompilerParams(
            collective_id=0, has_side_effects=True, vmem_limit_bytes=60 * 1024 * 1024
        ),
        name="filter_panel",
    )(
        orbitals,
        potential.reshape(cell_count // 128, 128),
        projector_atom.reshape(1, entries),
        projector_cell.reshape(1, entries),
        projector_value.reshape(1, entries),
        atom_strength.reshape(1, -1),
        jnp.asarray(depth_band()),
        jnp.asarray(plane_bands()),
    )
    step_count, panel_rows, columns_out = ritz_rotation.shape
    chosen = (panel_owner[:, None] == jnp.arange(panels)[None, :]).astype(FLOAT)
    full = jnp.sum(
        ritz_rotation.astype(FLOAT).transpose(2, 0, 1)[:, :, None, :] * chosen[None, :, :, None], axis=1
    ).reshape(columns_out, panels * panel_rows)
    rounded = lax.reduce_precision(full, 8, 7)
    own_rotation = jnp.concatenate([rounded, full - rounded], 1).astype(HALF)
    halves, owners, planes, inner = np.meshgrid(
        np.arange(2), np.arange(panels), np.arange(DEPTH), np.arange(PANEL), indexing="ij"
    )
    spread_index = (halves * panels * PANEL + owners * PANEL + inner).reshape(1, -1).astype(np.int32)
    spread_plane = planes.reshape(1, -1).astype(np.int32)
    span = spread_index.shape[1]
    width = PLANE // panels
    piece = width // PIECES
    rotated = pl.pallas_call(
        functools.partial(rotate_kernel, panels),
        out_shape=jax.ShapeDtypeStruct((columns_out, cell_count), HALF),
        in_specs=[anywhere, in_vmem, in_vmem, in_vmem],
        out_specs=anywhere,
        scratch_shapes=[
            pltpu.VMEM((panels * columns_out, own_rotation.shape[1]), HALF),
            pltpu.VMEM((panels * columns_out * DEPTH, span), HALF),
            pltpu.VMEM((PIECES, panels * ROWS, piece), HALF),
            pltpu.VMEM((PIECES, panels * columns_out * DEPTH, piece), HALF),
            pltpu.VMEM((columns_out * DEPTH, PLANE), HALF),
            dma((DEPTH,)),
            dma((panels - 1,)),
            dma((panels - 1,)),
            dma((PIECES, panels - 1)),
            dma((PIECES, panels - 1)),
            dma((PIECES, panels - 1)),
            dma((PIECES, panels - 1)),
        ],
        compiler_params=pltpu.CompilerParams(
            collective_id=1, has_side_effects=True, vmem_limit_bytes=60 * 1024 * 1024
        ),
        name="rotate_panels",
    )(filtered_rows, own_rotation, jnp.asarray(spread_index), jnp.asarray(spread_plane))
    return (filtered, rotated)


def solution(mesh):
    in_specs = (
        P("orb", "grid"),
        P("grid"),
        P("grid"),
        P("grid"),
        P("grid"),
        P(),
        P(None, None, "orb"),
        P(),
    )
    out_specs = (P("orb", "grid"), P("orb", "grid"))
    local = functools.partial(body, mesh.shape["grid"], mesh.shape["orb"])
    return jax.shard_map(local, mesh=mesh, in_specs=in_specs, out_specs=out_specs, check_vma=False)
```

```python
import functools

import jax
import jax.numpy as jnp
import ml_dtypes
import numpy as np
from jax import lax
from jax.experimental import pallas as pl
from jax.experimental.pallas import tpu as pltpu
from jax.sharding import PartitionSpec as P

NX = 96
NY = 96
REACH = 6
ATOM_DEV = 4
PLANE = NX * NY
DEPTH = 6
PANEL = 8
ROWS = DEPTH * PANEL
BLOCK = 256
BLOCKS = PLANE // BLOCK
STRIP = 1024
LANES = 128
PAD = 640
WINDOW = BLOCK + 2 * PAD
PHASES = 3
CHUNKS = 3
CHUNK = PLANE // CHUNKS
CHUNK_STRIPS = CHUNK // STRIP
ATOM_SLOTS = 3 * ATOM_DEV
TABLE = 80
COARSE = 512
GROUPS_PER_TURN = 6
FLOAT = jnp.float32
HALF = jnp.bfloat16
MESH = pl.DeviceIdType.MESH

stencil_weights = (
    -5369.0 / 1800.0,
    12.0 / 7.0,
    -15.0 / 56.0,
    10.0 / 189.0,
    -1.0 / 112.0,
    2.0 / 1925.0,
    -1.0 / 16632.0,
)
cheb_center = 6.0
cheb_half = 6.0
unit = stencil_weights[1]


def plane_bands():
    bands = np.zeros((PHASES, WINDOW, BLOCK), np.float32)
    for phase in range(PHASES):
        target = phase * BLOCK + np.arange(BLOCK)
        source = phase * BLOCK - PAD + np.arange(WINDOW)
        jump = source[:, None] - target[None, :]
        same_row = (source[:, None] // NX) == (target[None, :] // NX)
        for k in range(1, REACH + 1):
            weight = stencil_weights[k] / unit
            bands[phase] += weight * ((np.abs(jump) == k) & same_row)
            bands[phase] += weight * (np.abs(jump) == k * NX)
    return bands.astype(ml_dtypes.bfloat16)


def depth_band():
    band = np.zeros((DEPTH, 3 * DEPTH), np.float32)
    for z in range(DEPTH):
        for k in range(1, REACH + 1):
            band[z, DEPTH + z - k] += stencil_weights[k] / unit
            band[z, DEPTH + z + k] += stencil_weights[k] / unit
    return np.kron(band, np.eye(PANEL, dtype=np.float32))


def contract_last(left, right):
    return lax.dot_general(left, right, (((1,), (1,)), ((), ())), preferred_element_type=FLOAT)


def dot(left, right):
    return jnp.dot(left, right, preferred_element_type=FLOAT)


def fused_kernel(
    slabs,
    panels,
    owners,
    orbitals,
    potential,
    atom,
    cell,
    value,
    strength,
    own_rotation,
    column_facts,
    depth_weights,
    bands_hbm,
    filtered,
    rotated,
    bands,
    stack,
    padded,
    planar,
    step,
    picks,
    spots,
    table,
    found_sums,
    sums_out,
    sums_in,
    rows_out,
    rotations,
    wide,
    gathered,
    products,
    landed,
    band_sem,
    halo_send,
    halo_recv,
    sums_send,
    sums_recv,
    local_sem,
    rot_send,
    rot_recv,
    in_send,
    in_recv,
    out_send,
    out_recv,
):
    me = lax.axis_index("grid")
    seat = lax.axis_index("orb")
    after, before = lax.rem(me + 1, slabs), lax.rem(me + slabs - 1, slabs)
    after2, before2 = lax.rem(me + 2, slabs), lax.rem(me + slabs - 2, slabs)
    others = [lax.rem(seat + k, panels) for k in range(1, panels)]
    barrier = pltpu.get_barrier_semaphore()
    for other in (after, before, after2, before2):
        pl.semaphore_signal(barrier, inc=1, device_id={"grid": other}, device_id_type=MESH)
    for other in others:
        pl.semaphore_signal(barrier, inc=1, device_id={"orb": other}, device_id_type=MESH)
    band_copy = pltpu.make_async_copy(bands_hbm, bands, band_sem)
    band_copy.start()

    def strip(j):
        return pl.ds(pl.multiple_of(j * STRIP, STRIP), STRIP)

    def at(index, size):
        return pl.ds(pl.multiple_of(index * size, size), size)

    def halo_copies(stage, chunk):
        columns = pl.ds(chunk * CHUNK, CHUNK)
        own = stack.at[stage, pl.ds(ROWS, ROWS), columns]
        return [
            pltpu.make_async_remote_copy(
                src_ref=own,
                dst_ref=stack.at[stage, pl.ds(place, ROWS), columns],
                send_sem=halo_send.at[stage, side, chunk],
                recv_sem=halo_recv.at[stage, side, chunk],
                device_id={"grid": other},
                device_id_type=MESH,
            )
            for side, (other, place) in enumerate(((after, 0), (before, 2 * ROWS)))
        ]

    def store_own(stage, j, rows):
        stack[stage, pl.ds(ROWS, ROWS), strip(j)] = rows
        padded[stage, :, pl.ds(pl.multiple_of(PAD + j * STRIP, LANES), STRIP)] = rows

    for chunk in range(CHUNKS):

        def take_block(i, carry, chunk=chunk):
            j = chunk * CHUNK_STRIPS + i
            planes = [
                orbitals[:, pl.ds(pl.multiple_of(z * PLANE + j * STRIP, STRIP), STRIP)].astype(FLOAT)
                for z in range(DEPTH)
            ]
            store_own(0, j, jnp.concatenate(planes, 0).astype(HALF))
            return carry

        lax.fori_loop(0, CHUNK_STRIPS, take_block, 0)
        if chunk == 0:
            pl.semaphore_wait(barrier, 4 + panels - 1)
        for copy in halo_copies(0, chunk):
            copy.start()

    rotation_copies = [
        pltpu.make_async_remote_copy(
            src_ref=own_rotation,
            dst_ref=rotations.at[seat],
            send_sem=rot_send.at[k],
            recv_sem=rot_recv.at[k],
            device_id={"orb": other},
            device_id_type=MESH,
        )
        for k, other in enumerate(others)
    ]
    for copy in rotation_copies:
        copy.start()
    rotations[seat] = own_rotation[...]
    for stage in range(2):
        padded[stage, :, pl.ds(0, PAD)] = jnp.zeros((ROWS, PAD), HALF)
        padded[stage, :, pl.ds(PAD + PLANE, PAD)] = jnp.zeros((ROWS, PAD), HALF)

    def as_row(ref):
        return jnp.concatenate([ref[i : i + 1, :] for i in range(ref.shape[0])], 1)

    cells = as_row(cell)
    plane_of = jnp.zeros_like(cells)
    for z in range(1, DEPTH):
        plane_of = plane_of + (cells >= z * PLANE).astype(jnp.int32)
    in_plane = cells - plane_of * PLANE
    slot = as_row(atom) - (me - 1) * ATOM_DEV
    coarse_key = (in_plane >> 9) * TABLE + plane_of * ATOM_SLOTS + slot
    fine_key = in_plane & (COARSE - 1)
    entries = cells.shape[1]
    values = as_row(value)
    high = values.astype(HALF).astype(FLOAT)
    low = values - high

    def fill_spots(i, carry):
        row = pl.multiple_of(i * 32, 32)
        here = (lax.broadcasted_iota(jnp.int32, (32, entries), 0) + row) == fine_key
        spots[pl.ds(row, 32), :] = jnp.where(here, high, 0.0).astype(HALF)
        spots[pl.ds(row + COARSE, 32), :] = jnp.where(here, low, 0.0).astype(HALF)
        return carry

    lax.fori_loop(0, COARSE // 32, fill_spots, 0)
    groups = PLANE // COARSE
    picked = GROUPS_PER_TURN * TABLE

    def fill_table(turn, carry):
        def fill_picks(i, inner):
            row = pl.multiple_of(i * 32, 32)
            here = (
                lax.broadcasted_iota(jnp.int32, (32, entries), 0) + (row + turn * picked)
            ) == coarse_key
            picks[pl.ds(row, 32), :] = jnp.where(here, 1.0, 0.0).astype(HALF)
            return inner

        lax.fori_loop(0, picked // 32, fill_picks, 0)
        full = contract_last(picks[...], spots[pl.ds(0, COARSE), :]) + contract_last(
            picks[...], spots[pl.ds(COARSE, COARSE), :]
        )
        for i in range(GROUPS_PER_TURN):
            part = full[i * TABLE : (i + 1) * TABLE]
            rounded = part.astype(HALF)
            columns = pl.ds(pl.multiple_of((turn * GROUPS_PER_TURN + i) * COARSE, COARSE), COARSE)
            table[pl.ds(0, TABLE), columns] = rounded
            table[pl.ds(TABLE, TABLE), columns] = (part - rounded.astype(FLOAT)).astype(HALF)
        return carry

    lax.fori_loop(0, groups // GROUPS_PER_TURN, fill_table, 0)

    lanes = lax.broadcasted_iota(jnp.int32, (PANEL, LANES), 1)
    near_strength = pltpu.roll(
        jnp.broadcast_to(strength[...], (PANEL, LANES)),
        lax.rem(LANES + ATOM_DEV - me * ATOM_DEV, LANES),
        1,
    )
    column_of = lax.broadcasted_iota(jnp.int32, (ROWS, 3 * ROWS), 1)
    has_before = (me > 0).astype(FLOAT)
    has_after = (me < slabs - 1).astype(FLOAT)
    keep = jnp.where(
        column_of < ROWS, has_before, jnp.where(column_of >= 2 * ROWS, has_after, 1.0)
    )
    across = (depth_weights[...] * keep).astype(HALF)
    plane_lanes = [(lanes >= z * ATOM_SLOTS) & (lanes < (z + 1) * ATOM_SLOTS) for z in range(DEPTH)]
    partners = ((after, LANES - 4), (before, 4), (after2, LANES - 8), (before2, 8))
    found_sums[...] = jnp.zeros((ROWS, LANES), FLOAT)
    slot_row = lax.broadcasted_iota(jnp.int32, (LANES, 2 * TABLE), 0)
    slot_column = lax.broadcasted_iota(jnp.int32, (LANES, 2 * TABLE), 1)
    to_high = slot_row == slot_column
    to_both = to_high | (slot_row + TABLE == slot_column)
    to_high = jnp.where(to_high & (slot_row < TABLE), 1.0, 0.0).astype(HALF)
    to_both = jnp.where(to_both & (slot_row < TABLE), 1.0, 0.0).astype(HALF)

    def send_sums(stage):
        field = stack[stage, pl.ds(ROWS, ROWS), :]
        found_sums[:, pl.ds(0, TABLE)] = contract_last(
            field, table[pl.ds(0, TABLE), :]
        ) + contract_last(field, table[pl.ds(TABLE, TABLE), :])
        both = found_sums[...]
        own = jnp.zeros((PANEL, LANES), FLOAT)
        for z in range(DEPTH):
            part = jnp.where(plane_lanes[z], both[z * PANEL : (z + 1) * PANEL], 0.0)
            own = own + (part if z == 0 else pltpu.roll(part, LANES - z * ATOM_SLOTS, 1))
        sums_out[stage] = own
        copies = [
            pltpu.make_async_remote_copy(
                src_ref=sums_out.at[stage],
                dst_ref=sums_in.at[stage, k],
                send_sem=sums_send.at[stage, k],
                recv_sem=sums_recv.at[stage, k],
                device_id={"grid": other},
                device_id_type=MESH,
            )
            for k, (other, _) in enumerate(partners)
        ]
        for copy in copies:
            copy.start()
        return copies

    def planar_part(stage):
        for phase in range(PHASES):
            windows = [
                padded[stage, :, pl.ds((i * PHASES + phase) * BLOCK, WINDOW)]
                for i in range(BLOCKS // PHASES)
            ]
            product = dot(jnp.concatenate(windows, 0), bands[phase])
            for i in range(BLOCKS // PHASES):
                planar[:, pl.ds((i * PHASES + phase) * BLOCK, BLOCK)] = product[
                    i * ROWS : (i + 1) * ROWS
                ]

    def coupling(stage, copies):
        for copy in copies:
            copy.wait()
        total = sums_out[stage]
        for k, (_, turn) in enumerate(partners):
            total = total + pltpu.roll(sums_in[stage, k], turn, 1)
        scaled = jnp.where(plane_lanes[0], total * near_strength, 0.0)
        blocks = [
            scaled if z == 0 else pltpu.roll(scaled, z * ATOM_SLOTS, 1) for z in range(DEPTH)
        ]
        spread = jnp.concatenate(blocks, 0)
        rounded = spread.astype(HALF)
        rest = (spread - rounded.astype(FLOAT)).astype(HALF)
        return jnp.concatenate([dot(rounded, to_both), dot(rest, to_high)], 0).astype(HALF)

    def image(stage, j, couplings, middle):
        columns = strip(j)
        neighbours = planar[:, columns] + dot(across, stack[stage, :, columns])
        both = dot(couplings, table[:, columns])
        rows = []
        for z in range(DEPTH):
            pieces = [
                jnp.broadcast_to(
                    potential[pl.ds(z * (PLANE // LANES) + j * (STRIP // LANES) + h, 1), :],
                    (PANEL, LANES),
                )
                for h in range(STRIP // LANES)
            ]
            rows.append(jnp.concatenate(pieces, 1))
        local = (jnp.concatenate(rows, 0) - (1.5 * stencil_weights[0] + cheb_center)) * (
            1.0 / cheb_half
        )
        return (
            middle * local
            - (0.5 * unit / cheb_half) * neighbours
            + (both[:ROWS] + both[ROWS:]) * (1.0 / cheb_half)
        )

    sums = send_sums(0)
    band_copy.wait()
    planar_part(0)
    couplings = coupling(0, sums)
    for chunk in range(CHUNKS):
        for copy in halo_copies(0, chunk):
            copy.wait()

        def first_block(i, carry, chunk=chunk):
            j = chunk * CHUNK_STRIPS + i
            middle = stack[0, pl.ds(ROWS, ROWS), strip(j)].astype(FLOAT)
            field = image(0, j, couplings, middle)
            step[:, strip(j)] = field
            store_own(1, j, field.astype(HALF))
            return carry

        lax.fori_loop(0, CHUNK_STRIPS, first_block, 0)
        for copy in halo_copies(1, chunk):
            copy.start()

    sums = send_sums(1)
    planar_part(1)

    for copy in rotation_copies:
        copy.wait()
    inputs, columns_out = own_rotation.shape
    target = lax.broadcasted_iota(jnp.int32, (panels * columns_out, columns_out), 0)
    member = lax.broadcasted_iota(jnp.int32, (panels * columns_out, columns_out), 1)
    every = jnp.zeros((panels * columns_out, inputs), FLOAT)
    for d in range(panels):
        place = jnp.where(target == member + d * columns_out, 1.0, 0.0).astype(HALF)
        every = every + contract_last(place, rotations[d])
    every = every.astype(HALF)
    span = panels * ROWS
    input_of = lax.broadcasted_iota(jnp.int32, (inputs, span), 0)
    owner_of = jnp.zeros((inputs, span), jnp.int32)
    for s in range(inputs // PANEL):
        inside = (input_of >= s * PANEL) & (input_of < (s + 1) * PANEL)
        owner_of = owner_of + jnp.where(inside, owners[s], 0)
    matches = (owner_of == column_facts[0:1, :]) & (
        (input_of & (PANEL - 1)) == column_facts[2:3, :]
    )
    for z in range(DEPTH):
        chosen = jnp.where(matches & (column_facts[1:2, :] == z), 1.0, 0.0).astype(HALF)
        product = dot(every, chosen)
        rounded = product.astype(HALF)
        rest = (product - rounded.astype(FLOAT)).astype(HALF)
        for d in range(panels):
            place = pl.ds((d * DEPTH + z) * columns_out, columns_out)
            wide[place, pl.ds(0, span)] = rounded[d * columns_out : (d + 1) * columns_out]
            wide[place, pl.ds(span, span)] = rest[d * columns_out : (d + 1) * columns_out]

    piece = CHUNK // panels
    deep = DEPTH * columns_out

    def columns_of(owner, chunk):
        return pl.ds(pl.multiple_of(owner * piece + chunk * CHUNK, LANES), piece)

    def panel_copies(chunk):
        return [
            pltpu.make_async_remote_copy(
                src_ref=rows_out.at[:, columns_of(other, chunk)],
                dst_ref=gathered.at[chunk, at(seat, ROWS), :],
                send_sem=in_send.at[chunk, k],
                recv_sem=in_recv.at[chunk, k],
                device_id={"orb": other},
                device_id_type=MESH,
            )
            for k, other in enumerate(others)
        ]

    couplings = coupling(1, sums)
    for chunk in range(CHUNKS):
        for copy in halo_copies(1, chunk):
            copy.wait()

        def second_block(i, carry, chunk=chunk):
            j = chunk * CHUNK_STRIPS + i
            initial = stack[0, pl.ds(ROWS, ROWS), strip(j)].astype(FLOAT)
            field = 2.0 * image(1, j, couplings, step[:, strip(j)]) - initial
            rows_out[:, strip(j)] = field.astype(HALF)
            return carry

        lax.fori_loop(0, CHUNK_STRIPS, second_block, 0)
        for copy in panel_copies(chunk):
            copy.start()
        gathered[chunk, at(seat, ROWS), :] = rows_out[:, columns_of(seat, chunk)]
    filtered_backs = [
        pltpu.make_async_copy(
            rows_out.at[pl.ds(z * PANEL, PANEL), :],
            filtered.at[:, pl.ds(z * PLANE, PLANE)],
            local_sem.at[0, z],
        )
        for z in range(DEPTH)
    ]
    for copy in filtered_backs:
        copy.start()

    result_copies = []
    for chunk in range(CHUNKS):
        for copy in panel_copies(chunk):
            copy.wait()
        operand = gathered[chunk]
        product = dot(wide[:, pl.ds(0, span)], operand) + dot(wide[:, pl.ds(span, span)], operand)
        products[chunk] = product.astype(HALF)
        copies = [
            pltpu.make_async_remote_copy(
                src_ref=products.at[chunk, at(other, deep), :],
                dst_ref=landed.at[:, columns_of(seat, chunk)],
                send_sem=out_send.at[chunk, k],
                recv_sem=out_recv.at[chunk, k],
                device_id={"orb": other},
                device_id_type=MESH,
            )
            for k, other in enumerate(others)
        ]
        for copy in copies:
            copy.start()
        landed[:, columns_of(seat, chunk)] = products[chunk, at(seat, deep), :]
        result_copies.extend(copies)
    for copy in filtered_backs:
        copy.wait()
    for copy in result_copies:
        copy.wait()
    rotated_backs = [
        pltpu.make_async_copy(
            landed.at[pl.ds(z * columns_out, columns_out), :],
            rotated.at[:, pl.ds(z * PLANE, PLANE)],
            local_sem.at[1, z],
        )
        for z in range(DEPTH)
    ]
    for copy in rotated_backs:
        copy.start()
    for copy in rotated_backs:
        copy.wait()


def body(
    slabs,
    panels,
    orbitals,
    potential,
    projector_atom,
    projector_cell,
    projector_value,
    atom_strength,
    ritz_rotation,
    panel_owner,
):
    cell_count = orbitals.shape[1]
    entries = projector_atom.shape[0]
    steps, panel_rows, columns_out = ritz_rotation.shape
    in_vmem = pl.BlockSpec(memory_space=pltpu.VMEM)
    anywhere = pl.BlockSpec(memory_space=pl.ANY)
    dma = pltpu.SemaphoreType.DMA
    owner, plane, inner = np.meshgrid(
        np.arange(panels), np.arange(DEPTH), np.arange(PANEL), indexing="ij"
    )
    column_facts = np.zeros((8, panels * ROWS), np.int32)
    column_facts[:3] = [owner.ravel(), plane.ravel(), inner.ravel()]
    piece = CHUNK // panels
    deep = DEPTH * columns_out
    return pl.pallas_call(
        functools.partial(fused_kernel, slabs, panels),
        out_shape=(
            jax.ShapeDtypeStruct(orbitals.shape, HALF),
            jax.ShapeDtypeStruct((columns_out, cell_count), HALF),
        ),
        in_specs=[pl.BlockSpec(memory_space=pltpu.SMEM)] + [in_vmem] * 9 + [anywhere],
        out_specs=(anywhere, anywhere),
        scratch_shapes=[
            pltpu.VMEM((PHASES, WINDOW, BLOCK), HALF),
            pltpu.VMEM((2, 3 * ROWS, PLANE), HALF),
            pltpu.VMEM((2, ROWS, PLANE + 2 * PAD), HALF),
            pltpu.VMEM((ROWS, PLANE), FLOAT),
            pltpu.VMEM((ROWS, PLANE), FLOAT),
            pltpu.VMEM((GROUPS_PER_TURN * TABLE, entries), HALF),
            pltpu.VMEM((2 * COARSE, entries), HALF),
            pltpu.VMEM((2 * TABLE, PLANE), HALF),
            pltpu.VMEM((ROWS, LANES), FLOAT),
            pltpu.VMEM((2, PANEL, LANES), FLOAT),
            pltpu.VMEM((2, 4, PANEL, LANES), FLOAT),
            pltpu.VMEM((ROWS, PLANE), HALF),
            pltpu.VMEM((panels, steps * panel_rows, columns_out), HALF),
            pltpu.VMEM((panels * deep, 2 * panels * ROWS), HALF),
            pltpu.VMEM((CHUNKS, panels * ROWS, piece), HALF),
            pltpu.VMEM((CHUNKS, panels * deep, piece), HALF),
            pltpu.VMEM((deep, PLANE), HALF),
            dma,
            dma((2, 2, CHUNKS)),
            dma((2, 2, CHUNKS)),
            dma((2, 4)),
            dma((2, 4)),
            dma((2, DEPTH)),
            dma((panels - 1,)),
            dma((panels - 1,)),
            dma((CHUNKS, panels - 1)),
            dma((CHUNKS, panels - 1)),
            dma((CHUNKS, panels - 1)),
            dma((CHUNKS, panels - 1)),
        ],
        compiler_params=pltpu.CompilerParams(
            collective_id=0, has_side_effects=True, vmem_limit_bytes=60 * 1024 * 1024
        ),
        name="fused_filter",
    )(
        panel_owner,
        orbitals,
        potential.reshape(cell_count // LANES, LANES),
        projector_atom.reshape(entries // LANES, LANES),
        projector_cell.reshape(entries // LANES, LANES),
        projector_value.reshape(entries // LANES, LANES),
        atom_strength.reshape(1, -1),
        ritz_rotation.reshape(steps * panel_rows, columns_out),
        jnp.asarray(column_facts),
        jnp.asarray(depth_band()),
        jnp.asarray(plane_bands()),
    )


def solution(mesh):
    in_specs = (
        P("orb", "grid"),
        P("grid"),
        P("grid"),
        P("grid"),
        P("grid"),
        P(),
        P(None, None, "orb"),
        P(),
    )
    out_specs = (P("orb", "grid"), P("orb", "grid"))
    local = functools.partial(body, mesh.shape["grid"], mesh.shape["orb"])
    return jax.shard_map(local, mesh=mesh, in_specs=in_specs, out_specs=out_specs, check_vma=False)
```
